256 devices in a mesh: ev: 64 (over y, z_lo, x, core), sys: 4 (over z_hi).
Axes of the slice: x: 4, y: 4, z: 8 (z_hi: 4, z_lo: 2; z = z_hi * 2 + z_lo), core: 2. Of those that a mesh axis runs over, the one named last changes fastest.
Arguments:
- observables: bfloat16 [32768, 512], P('ev'), may hold values from -6 to 6
- selection: int32 [32768, 512], P('ev'), may hold values 0 or 1
- base_weight: float32 [32768], P('ev'), may hold values from 0.05 to 0.5
- category: int32 [32768], P('ev'), may hold values from 0 to 63
- bin_number: int32 [32768], P('ev'), may hold values from 0 to 255
- response: bfloat16 [512, 512], P(None, 'sys'), may hold values from -0.25 to 0.25
- nuisance_pulls: float32 [256], P('sys'), may hold values from -2 to 2
Outputs:
- templates: float32 [64, 512, 256], P('ev', 'sys')
- expected: float32 [64, 256], P('ev')
The draws below stay inside these ranges and needn't reach their ends.
All inputs are finite; a program needn't handle non-finite values. No bound on the sum of `selection` on one device may be relied on, other than what follows from the above.
Results may differ from the reference program's by a relative error of at most 0.0003.
Values sent between devices are 32-bit elements; how exact they have to be, the bound alone decides.
A program may use at most 64 MiB of HBM per device.

```python
import math
import jax
import jax.numpy as jnp

C = 64
B = 256
NUIS = 256
NP = 512
S = 512
EVENTS = 32768


def with_ends(values, stream_key, smallest, high):
    index_at = [jax.random.randint(jax.random.fold_in(stream_key, axis), (), 0, length) for axis, length in enumerate(values.shape)]
    longest = values.shape.index(max(values.shape))
    neighbour = index_at[:longest] + [(index_at[longest] + 1) % values.shape[longest]] + index_at[longest + 1:]
    return values.at[tuple(index_at)].set(smallest).at[tuple(neighbour)].set(high)


def block_levels(key, dims, split, least, high):
    factor_of = 1.0
    for axis_at, parts in split:
        heights = jax.random.uniform(jax.random.fold_in(jax.random.fold_in(key, 6), axis_at), (parts,), jnp.float32, least / len(split), high / len(split))
        factor_of = factor_of * jnp.repeat(jnp.exp(heights), dims[axis_at] // parts).reshape((-1,) + (1,) * (len(dims) - 1 - axis_at))
    return factor_of


def gaussian(key, shape, width, most, shards=(), dtype=jnp.bfloat16):
    gain = block_levels(key, shape, shards, -0.22, 0.18) if shards else 1.0
    array = jax.random.normal(key, shape, jnp.float32) * width * gain
    return jnp.minimum(jnp.maximum(array, -most), most).astype(dtype)


def setup_inputs(seed: int = 0) -> dict:
    seeds = jax.random.split(jax.random.key(seed), 8)
    return {
        "observables": gaussian(seeds[0], (EVENTS, NP), 1.0, 6.0, ((0, 64),)),
        "selection": with_ends((jax.random.randint(seeds[1], (EVENTS, NP), 0, 2) < 1).astype(jnp.int32), jax.random.fold_in(seeds[1], 1), 0, 1),
        "base_weight": jnp.clip(jnp.exp(math.log(0.5) - 2.3025851 * jax.random.uniform(seeds[2], (EVENTS,), jnp.float32) ** block_levels(seeds[2], (EVENTS,), ((0, 64),), -0.2, 0.2)), 0.05, 0.5),
        "category": with_ends(jax.random.randint(seeds[3], (EVENTS,), 0, C), jax.random.fold_in(seeds[3], 1), 0, C - 1).astype(jnp.int32),
        "bin_number": with_ends(jax.random.randint(seeds[4], (EVENTS,), 0, B), jax.random.fold_in(seeds[4], 1), 0, B - 1).astype(jnp.int32),
        "response": gaussian(seeds[5], (NP, S), NP ** -0.5, 0.25, ((1, 4),)),
        "nuisance_pulls": jnp.clip(jax.random.uniform(seeds[6], (NUIS,), jnp.float32, -2.0, 2.0) * block_levels(seeds[6], (NUIS,), ((0, 4),), -0.4, 0.0), -2.0, 2.0),
    }


def reference(observables, selection, base_weight, category, bin_number, response, nuisance_pulls):
    masked = observables * selection.astype(jnp.bfloat16)
    log_shift = jnp.dot(masked, response, preferred_element_type=jnp.float32)
    variation_weight = base_weight[:, None] * jnp.exp(0.2 * log_shift)
    flat_index = (category * B + bin_number).astype(jnp.int32)
    summed = jax.ops.segment_sum(variation_weight, flat_index, num_segments=C * B)
    templates = jnp.transpose(summed.reshape(C, B, 2 * NUIS), (0, 2, 1))
    nominal = jax.ops.segment_sum(base_weight, flat_index, num_segments=C * B).reshape(C, B)
    upward = templates[:, 0::2, :]
    downward = templates[:, 1::2, :]
    pull_col = nuisance_pulls[None, :, None]
    nominal_col = nominal[:, None, :]
    changes = jnp.where(pull_col >= 0.0, pull_col * (upward - nominal_col), pull_col * (nominal_col - downward))
    expected = nominal + jnp.sum(changes, axis=1)
    return templates, expected
```

```python
import functools

import jax
import jax.numpy as jnp
from jax import lax
from jax.experimental import pallas as pl
from jax.experimental.pallas import tpu as pltpu
from jax.sharding import PartitionSpec as P

B = 256
K = 24
U_LANE = 32
N_LANE = 64
MESH = pl.DeviceIdType.MESH
F32 = jnp.float32
BF16 = jnp.bfloat16


def iota(shape, dim):
    return lax.broadcasted_iota(jnp.int32, shape, dim)


def onehot(mask):
    return jnp.where(mask, 1.0, 0.0).astype(BF16)


def parts(x, count):
    out = []
    for _ in range(count):
        piece = x.astype(BF16)
        out.append(piece)
        x = x - piece.astype(F32)
    return out


def dot(a, b):
    return jnp.dot(a, b, preferred_element_type=F32)


def dot_nt(a, b):
    return lax.dot_general(a, b, (((1,), (1,)), ((), ())), preferred_element_type=F32)


def exchange(n_ev, n_sys, later, *refs):
    if later:
        round_ref, *refs = refs
    (
        obs_hbm, sel_hbm, base_ref, cat_ref, bin_ref, resp_ref, pull_ref,
        hist_ref, expected_ref, most_ref,
        obs, sel, weight, send, recv, meta, meta_in, u_all,
        load_sem, u_send_sem, u_recv_sem, send_sem, recv_sem, meta_send_sem, meta_recv_sem,
    ) = refs
    events, features = obs.shape
    variations = weight.shape[1]
    me, my_sys = lax.axis_index("ev"), lax.axis_index("sys")
    steps = 4
    rows = events // steps

    loads = []
    for i in range(steps):
        part = pl.ds(i * rows, rows)
        loads.append((
            pltpu.make_async_copy(obs_hbm.at[part], obs.at[part], load_sem.at[0, i]),
            pltpu.make_async_copy(sel_hbm.at[part], sel.at[part], load_sem.at[1, i]),
        ))
        for load in loads[-1]:
            load.start()

    barrier = pltpu.get_barrier_semaphore()

    def greet(d, carry):
        pl.semaphore_signal(
            barrier, inc=1, device_id={"ev": lax.rem(me + d, n_ev)}, device_id_type=MESH
        )
        return carry

    lax.fori_loop(1, n_ev, greet, 0)
    for q in range(1, n_sys):
        pl.semaphore_signal(
            barrier, inc=1, device_id={"sys": lax.rem(my_sys + q, n_sys)}, device_id_type=MESH
        )

    cat = cat_ref[...]
    in_channel = iota((n_ev, events), 0) == cat
    before = onehot(iota((events, events), 0) < iota((events, events), 1))
    ahead = dot(onehot(in_channel), before)
    rank = jnp.sum(jnp.where(in_channel, ahead, 0.0), axis=0, keepdims=True)
    most = jnp.max(rank, axis=1, keepdims=True) + 1.0
    rank = rank.astype(jnp.int32)
    if later:
        rank = rank - round_ref[0] * K
    kept = jnp.logical_and(rank >= 0, rank < K)
    slot = jnp.where(kept, cat * K + rank, -1)
    rank = jnp.where(kept, rank, -1)

    base = base_ref[...]
    base_col = jnp.broadcast_to(base, (variations, events)).T
    for i in range(steps):
        part = pl.ds(i * rows, rows)
        for load in loads[i]:
            load.wait()
        masked = obs[part, :] * sel[part, :].astype(F32).astype(BF16)
        log_shift = dot(masked, resp_ref[...])
        weight[part, :] = base_col[i * rows : (i + 1) * rows] * jnp.exp(0.2 * log_shift)

    var_at = iota((variations, variations // 2), 0)
    mine = iota((variations, variations // 2), 1) == var_at // 2
    pull = jnp.sum(jnp.where(mine, pull_ref[...], 0.0), axis=1, keepdims=True)
    odd = iota((variations, 1), 0) % 2
    coef = jnp.maximum(jnp.where(odd == 0, pull, -pull), 0.0)
    w = weight[...]
    u_all[my_sys] = jnp.sum(coef * (w.T - base), axis=0, keepdims=True)

    pl.semaphore_wait(barrier, n_ev - 1 + n_sys - 1)

    u_copies = []
    for q in range(1, n_sys):
        u_copies.append(pltpu.make_async_remote_copy(
            src_ref=u_all.at[my_sys],
            dst_ref=u_all.at[my_sys],
            send_sem=u_send_sem.at[q],
            recv_sem=u_recv_sem.at[q],
            device_id={"sys": lax.rem(my_sys + q, n_sys)},
            device_id_type=MESH,
        ))
        u_copies[-1].start()

    halves = parts(w, 2)
    chunk = 4
    for i in range(chunk):
        count = n_ev * K // chunk
        pick = onehot(iota((count, events), 0) + i * count == slot)
        send[pl.ds(i * count, count), :] = sum(dot(pick, half) for half in halves)

    def row_copy(d):
        to = lax.rem(me + d, n_ev)
        return pltpu.make_async_remote_copy(
            src_ref=send.at[pl.ds(pl.multiple_of(to * K, 8), K)],
            dst_ref=recv.at[pl.ds(pl.multiple_of(d * K, 8), K)],
            send_sem=send_sem,
            recv_sem=recv_sem,
            device_id={"ev": to},
            device_id_type=MESH,
        )

    def send_rows(i, carry):
        row_copy(lax.rem(i * 27, n_ev)).start()
        return carry

    lax.fori_loop(1, n_ev, send_rows, 0)
    recv[pl.ds(0, K), :] = send[pl.ds(pl.multiple_of(me * K, 8), K), :]

    for copy in u_copies:
        copy.wait()
    u = base
    for q in range(n_sys):
        u = u + u_all[q]
    at_bin = onehot(iota((128, events), 0) == rank)
    at_u = onehot(iota((128, events), 0) - U_LANE == rank)
    row = dot_nt(jnp.where(in_channel, bin_ref[...].astype(F32), 0.0).astype(BF16), at_bin)
    for piece in parts(jnp.where(in_channel, u, 0.0), 3):
        row = row + dot_nt(piece, at_u)
    row = jnp.where(iota(row.shape, 1) >= N_LANE, most, row)
    meta[...] = row[:, None, :]

    def meta_copy(d):
        to = lax.rem(me + d, n_ev)
        return pltpu.make_async_remote_copy(
            src_ref=meta.at[to],
            dst_ref=meta_in.at[d],
            send_sem=meta_send_sem,
            recv_sem=meta_recv_sem,
            device_id={"ev": to},
            device_id_type=MESH,
        )

    def send_meta(i, carry):
        meta_copy(lax.rem(i * 27, n_ev)).start()
        return carry

    lax.fori_loop(1, n_ev, send_meta, 0)
    meta_in[0] = meta[me]

    others = pl.ds(1, n_ev - 1)
    all_meta = pltpu.make_async_remote_copy(
        src_ref=meta.at[others], dst_ref=meta_in.at[others], send_sem=meta_send_sem,
        recv_sem=meta_recv_sem, device_id={"ev": lax.rem(me + 1, n_ev)}, device_id_type=MESH,
    )
    all_meta.wait()
    got = meta_in[:, 0, :]
    most_ref[...] = jnp.max(got[:, N_LANE:], axis=0, keepdims=True)
    slots = n_ev * K
    at = iota((1, slots), 1).astype(F32)
    sender = jnp.floor((at + 0.5) * (1.0 / K))
    place = (at - K * sender).astype(jnp.int32)
    sender = sender.astype(jnp.int32)
    ours = iota((n_ev, slots), 0) == sender
    spread_bin = onehot(iota((128, slots), 0) == place)
    spread_u = onehot(iota((128, slots), 0) - U_LANE == place)
    pieces = parts(got, 3)
    bins = jnp.sum(jnp.where(ours, dot(pieces[0], spread_bin), 0.0), axis=0, keepdims=True)
    terms = sum(dot(piece, spread_u) for piece in pieces)
    terms = jnp.sum(jnp.where(ours, terms, 0.0), axis=0, keepdims=True)
    in_bin = iota((B, slots), 0) == bins.astype(jnp.int32)
    filled = jnp.sum(jnp.where(in_bin, terms, 0.0), axis=1, keepdims=True)
    expected_ref[...] = jnp.broadcast_to(filled, (B, 128)).T[0:1]

    some = pl.ds(K, (n_ev - 1) * K)
    all_rows = pltpu.make_async_remote_copy(
        src_ref=send.at[some], dst_ref=recv.at[some], send_sem=send_sem, recv_sem=recv_sem,
        device_id={"ev": lax.rem(me + 1, n_ev)}, device_id_type=MESH,
    )
    all_rows.wait()
    wide = jnp.concatenate(parts(recv[...], 2), axis=1)
    total = dot(onehot(in_bin), wide)
    hist_ref[...] = (total[:, :variations] + total[:, variations:]).T


def local(n_ev, n_sys, observables, selection, base_weight, category, bin_number, response, nuisance_pulls):
    events, features = observables.shape
    variations = response.shape[1]

    def call(later, *lead):
        vmem = pl.BlockSpec(memory_space=pltpu.VMEM)
        hbm = pl.BlockSpec(memory_space=pl.ANY)
        return pl.pallas_call(
            functools.partial(exchange, n_ev, n_sys, later),
            out_shape=(
                jax.ShapeDtypeStruct((variations, B), F32),
                jax.ShapeDtypeStruct((1, B), F32),
                jax.ShapeDtypeStruct((1, 128 - N_LANE), F32),
            ),
            in_specs=[pl.BlockSpec(memory_space=pltpu.SMEM)] * len(lead) + [hbm] * 2 + [vmem] * 5,
            out_specs=(vmem, vmem, vmem),
            scratch_shapes=[
                pltpu.VMEM((events, features), BF16),
                pltpu.VMEM((events, features), jnp.int32),
                pltpu.VMEM((events, variations), F32),
                pltpu.VMEM((n_ev * K, variations), F32),
                pltpu.VMEM((n_ev * K, variations), F32),
                pltpu.VMEM((n_ev, 1, 128), F32),
                pltpu.VMEM((n_ev, 1, 128), F32),
                pltpu.VMEM((n_sys, 1, events), F32),
                pltpu.SemaphoreType.DMA((2, 4)),
                pltpu.SemaphoreType.DMA((n_sys,)),
                pltpu.SemaphoreType.DMA((n_sys,)),
                pltpu.SemaphoreType.DMA,
                pltpu.SemaphoreType.DMA,
                pltpu.SemaphoreType.DMA,
                pltpu.SemaphoreType.DMA,
            ],
            compiler_params=pltpu.CompilerParams(
                collective_id=1 if later else 0, has_side_effects=True, vmem_limit_bytes=32 << 20
            ),
            name="later_round" if later else "first_round",
        )(
            *lead,
            observables,
            selection,
            base_weight.reshape(1, events),
            category.reshape(1, events),
            bin_number.reshape(1, events),
            response,
            nuisance_pulls.reshape(1, -1),
        )

    templates, expected, most = call(False)
    largest = most[0, 0].astype(jnp.int32)

    def more(carry):
        return carry[0] * K < largest

    def next_round(carry):
        index, templates, expected = carry
        extra, extra_expected, _ = call(True, index.reshape(1))
        return index + 1, templates + extra, expected + extra_expected

    _, templates, expected = lax.while_loop(more, next_round, (jnp.int32(1), templates, expected))
    return templates[None], expected


def solution(mesh):
    placed = (P("ev", None), P("ev", None), P("ev"), P("ev"), P("ev"), P(None, "sys"), P("sys"))
    return jax.shard_map(
        functools.partial(local, mesh.shape["ev"], mesh.shape["sys"]),
        mesh=mesh,
        in_specs=placed,
        out_specs=(P("ev", "sys", None), P("ev", None)),
        check_vma=False,
    )
```

```python
import functools

import jax
import jax.numpy as jnp
from jax import lax
from jax.experimental import pallas as pl
from jax.experimental.pallas import tpu as pltpu
from jax.sharding import PartitionSpec as P

B = 256
K = 24
STRIDE = 27
PACKS = 8
ARRIVALS = 4
FIRST_PACKS = 6
STEPS = 4
U_LANE = 32
N_LANE = 64
VMEM_BYTES = 48 << 20
MESH = pl.DeviceIdType.MESH
F32 = jnp.float32
BF16 = jnp.bfloat16


def iota(shape, dim):
    return lax.broadcasted_iota(jnp.int32, shape, dim)


def onehot(mask):
    return jnp.where(mask, 1.0, 0.0).astype(BF16)


def parts(x, count):
    out = []
    for _ in range(count):
        piece = x.astype(BF16)
        out.append(piece)
        x = x - piece.astype(F32)
    return out


def dot(a, b):
    return jnp.dot(a, b, preferred_element_type=F32)


def dot_nt(a, b):
    return lax.dot_general(a, b, (((1,), (1,)), ((), ())), preferred_element_type=F32)


def prepare(n_ev, me, hbm_refs, weight, info, vmem_refs, small_sem, load_sem, greet):
    obs_hbm, sel_hbm, base_hbm, cat_hbm, bin_hbm, resp_hbm = hbm_refs
    obs, sel, base_ref, cat_ref, bin_ref, resp_ref = vmem_refs
    events = obs.shape[0]
    variations = weight.shape[1]
    rows = events // STEPS

    small = []
    for i, (source, target) in enumerate((
        (cat_hbm, cat_ref), (bin_hbm, bin_ref), (base_hbm, base_ref), (resp_hbm, resp_ref),
    )):
        small.append(pltpu.make_async_copy(source, target, small_sem.at[i]))
        small[-1].start()
    loads = []
    for i in range(STEPS):
        part = pl.ds(i * rows, rows)
        loads.append((
            pltpu.make_async_copy(obs_hbm.at[part], obs.at[part], load_sem.at[0, i]),
            pltpu.make_async_copy(sel_hbm.at[part], sel.at[part], load_sem.at[1, i]),
        ))
        for load in loads[-1]:
            load.start()
    greet()

    before = onehot(iota((events, events), 0) < iota((events, events), 1))
    for copy in small:
        copy.wait()
    cat = cat_ref[...]
    away = jnp.where(cat < me, cat - me + n_ev, cat - me)
    block = away * pow(STRIDE, -1, n_ev) % n_ev
    in_block = iota((n_ev, events), 0) == block
    ahead = dot(onehot(in_block), before)
    rank = jnp.sum(jnp.where(in_block, ahead, 0.0), axis=0, keepdims=True)
    base = base_ref[...]
    info[0:1, :] = block.astype(F32)
    info[1:2, :] = rank
    info[2:3, :] = bin_ref[...].astype(F32)
    info[3:4, :] = base
    base_col = jnp.broadcast_to(base, (variations, events)).T

    for i in range(STEPS):
        part = pl.ds(i * rows, rows)
        for load in loads[i]:
            load.wait()
        masked = obs[part, :] * sel[part, :].astype(F32).astype(BF16)
        log_shift = dot(masked, resp_ref[...])
        weight[part, :] = base_col[i * rows : (i + 1) * rows] * jnp.exp(0.2 * log_shift)


def exchange(n_ev, n_sys, later, *refs):
    if later:
        (
            round_ref, weight, info, hist_ref, expected_ref,
            send, recv, meta, meta_in, picked, send_sem, recv_sem, meta_send_sem, meta_recv_sem,
        ) = refs
    else:
        hbm_refs, refs = refs[:6], refs[6:]
        (
            pull_hbm, hist_ref, expected_ref, most_ref, weight, info,
            send, recv, meta, meta_in, picked, send_sem, recv_sem, meta_send_sem, meta_recv_sem,
            share, pull_ref, small_sem, share_send_sem, share_recv_sem, *vmem_refs, load_sem,
        ) = refs
    events, variations = weight.shape
    slots = n_ev * K
    me, my_sys = lax.axis_index("ev"), lax.axis_index("sys")
    barrier = pltpu.get_barrier_semaphore()

    half = n_sys // 2
    first_half = my_sys < half

    def greet():
        def signal(d, carry):
            pl.semaphore_signal(
                barrier, inc=1, device_id={"ev": lax.rem(me + d, n_ev)}, device_id_type=MESH
            )
            return carry

        lax.fori_loop(1, n_ev, signal, 0, unroll=7 if n_ev == 64 else 1)
        if later:
            return
        for q in range(n_sys):
            @pl.when(jnp.logical_and(q != my_sys, jnp.logical_or(first_half, q >= half)))
            def _():
                pl.semaphore_signal(barrier, inc=1, device_id={"sys": q}, device_id_type=MESH)

    def share_copy(sender, target):
        return pltpu.make_async_remote_copy(
            src_ref=share.at[my_sys],
            dst_ref=share.at[my_sys],
            send_sem=share_send_sem.at[target],
            recv_sem=share_recv_sem.at[sender],
            device_id={"sys": target},
            device_id_type=MESH,
        )

    if later:
        greet()
        pl.semaphore_wait(barrier, n_ev - 1)
    else:
        pull_copy = pltpu.make_async_copy(pull_hbm, pull_ref, small_sem.at[4])
        pull_copy.start()
        prepare(n_ev, me, hbm_refs, weight, info, vmem_refs, small_sem, load_sem, greet)

        pull_copy.wait()
        var_at = iota((variations, variations // 2), 0)
        mine = iota((variations, variations // 2), 1) == var_at // 2
        pull = jnp.sum(jnp.where(mine, pull_ref[...], 0.0), axis=1, keepdims=True)
        odd = iota((variations, 1), 0) % 2
        coef = jnp.maximum(jnp.where(odd == 0, pull, -pull), 0.0)
        share[my_sys] = jnp.sum(coef * (weight[...].T - info[3:4, :]), axis=0, keepdims=True)
        pl.semaphore_wait(barrier, n_ev - 1 + jnp.where(first_half, half - 1, n_sys - 1))
        for q in range(n_sys):
            @pl.when(jnp.logical_and(q != my_sys, jnp.logical_or(my_sys >= half, q < half)))
            def _():
                share_copy(my_sys, q).start()

    block = info[0:1, :].astype(jnp.int32)
    rank_f = info[1:2, :]
    most = jnp.max(rank_f, axis=1, keepdims=True) + 1.0
    rank = rank_f.astype(jnp.int32)
    if later:
        rank = rank - round_ref[0] * K
    kept = jnp.logical_and(rank >= 0, rank < K)
    slot = jnp.where(kept, block * K + rank, -1)
    rank = jnp.where(kept, rank, -1)

    def to(i):
        return {"ev": lax.rem(me + STRIDE * i % n_ev, n_ev)}

    w = weight[...]
    halves = jnp.concatenate(parts(w, 2), axis=1)
    count = slots // PACKS
    blocks = n_ev // PACKS

    def pack(p):
        pick = onehot(iota((count, events), 0) + p * count == slot)
        both = dot(pick, halves)
        send[pl.ds(p * count, count), :] = both[:, :variations] + both[:, variations:]
        for i in range(p * blocks, (p + 1) * blocks):
            if i > 0:
                pltpu.make_async_remote_copy(
                    src_ref=send.at[pl.ds(i * K, K)],
                    dst_ref=recv.at[pl.ds(i * K, K)],
                    send_sem=send_sem,
                    recv_sem=recv_sem.at[i * ARRIVALS // n_ev],
                    device_id=to(i),
                    device_id_type=MESH,
                ).start()

    for p in range(FIRST_PACKS):
        pack(p)

    if not later:
        @pl.when(first_half)
        def _():
            for q in range(half, n_sys):
                share_copy(q, q).wait_recv()
                share_copy(my_sys, q).start()

        for q in range(n_sys):
            @pl.when(jnp.logical_and(q != my_sys, jnp.logical_or(my_sys >= half, q < half)))
            def _():
                share_copy(q, q).wait_recv()

        term = info[3:4, :]
        for q in range(n_sys):
            term = term + share[q]
        info[3:4, :] = term
    term = info[3:4, :]
    in_block = iota((n_ev, events), 0) == block
    at_bin = onehot(iota((128, events), 0) == rank)
    at_term = onehot(iota((128, events), 0) - U_LANE == rank)
    row = dot_nt(jnp.where(in_block, info[2:3, :], 0.0).astype(BF16), at_bin)
    for piece in parts(jnp.where(in_block, term, 0.0), 3):
        row = row + dot_nt(piece, at_term)
    row = jnp.where(iota(row.shape, 1) >= N_LANE, most, row)
    meta[...] = row[:, None, :]
    for i in range(1, n_ev):
        pltpu.make_async_remote_copy(
            src_ref=meta.at[i], dst_ref=meta_in.at[i], send_sem=meta_send_sem,
            recv_sem=meta_recv_sem, device_id=to(i), device_id_type=MESH,
        ).start()
    meta_in[0] = meta[0]

    for p in range(FIRST_PACKS, PACKS):
        pack(p)
    recv[pl.ds(0, K), :] = send[pl.ds(0, K), :]

    at = iota((1, slots), 1).astype(F32)
    sender = jnp.floor((at + 0.5) * (1.0 / K))
    place = (at - K * sender).astype(jnp.int32)
    ours = iota((n_ev, slots), 0) == sender.astype(jnp.int32)
    spread_bin = onehot(iota((128, slots), 0) == place)
    spread_term = onehot(iota((128, slots), 0) - U_LANE == place)

    others = pl.ds(1, n_ev - 1)
    pltpu.make_async_remote_copy(
        src_ref=meta.at[others], dst_ref=meta_in.at[others], send_sem=meta_send_sem,
        recv_sem=meta_recv_sem, device_id=to(1), device_id_type=MESH,
    ).wait()
    got = meta_in[:, 0, :]
    if not later:
        most_ref[...] = jnp.max(got[:, N_LANE:], axis=0, keepdims=True)
    pieces = parts(got, 3)
    bins = jnp.sum(jnp.where(ours, dot(pieces[0], spread_bin), 0.0), axis=0, keepdims=True)
    terms = sum(dot(piece, spread_term) for piece in pieces)
    terms = jnp.sum(jnp.where(ours, terms, 0.0), axis=0, keepdims=True)
    in_bin = iota((B, slots), 0) == bins.astype(jnp.int32)
    filled = jnp.sum(jnp.where(in_bin, terms, 0.0), axis=1, keepdims=True)
    expected_ref[...] = jnp.broadcast_to(filled, (B, 128)).T[0:1]
    picked[...] = onehot(in_bin)

    def arrive(a):
        first = max(a * n_ev // ARRIVALS, 1)
        some = pl.ds(first * K, ((a + 1) * n_ev // ARRIVALS - first) * K)
        pltpu.make_async_remote_copy(
            src_ref=send.at[some], dst_ref=recv.at[some], send_sem=send_sem,
            recv_sem=recv_sem.at[a], device_id=to(1), device_id_type=MESH,
        ).wait_recv()

    def filled_by(first, last):
        wide = jnp.concatenate(parts(recv[first:last, :], 2), axis=1)
        return dot(picked[:, first:last], wide)

    early = slots // ARRIVALS * (ARRIVALS - 1)
    for a in range(ARRIVALS - 1):
        arrive(a)
    total = filled_by(0, early)
    arrive(ARRIVALS - 1)
    total = total + filled_by(early, slots)
    hist_ref[...] = (total[:, :variations] + total[:, variations:]).T

    sent = pl.ds(K, slots - K)
    pltpu.make_async_remote_copy(
        src_ref=send.at[sent], dst_ref=recv.at[sent], send_sem=send_sem,
        recv_sem=recv_sem.at[0], device_id=to(1), device_id_type=MESH,
    ).wait_send()
    if not later:
        for q in range(n_sys):
            @pl.when(q != my_sys)
            def _():
                share_copy(my_sys, q).wait_send()


def in_hbm(x):
    return pltpu.with_memory_space_constraint(x, pltpu.HBM)


def store(hist_ref, expected_ref, templates_hbm, expected_hbm, sem):
    copies = (
        pltpu.make_async_copy(hist_ref, templates_hbm.at[0], sem.at[0]),
        pltpu.make_async_copy(expected_ref, expected_hbm, sem.at[1]),
    )
    for copy in copies:
        copy.start()
    for copy in copies:
        copy.wait()


def finish(templates, expected):
    vmem = pl.BlockSpec(memory_space=pltpu.VMEM)
    hbm = pl.BlockSpec(memory_space=pltpu.HBM)
    return pl.pallas_call(
        store,
        out_shape=(
            jax.ShapeDtypeStruct((1,) + templates.shape, F32),
            jax.ShapeDtypeStruct(expected.shape, F32),
        ),
        in_specs=[vmem] * 2,
        out_specs=(hbm, hbm),
        scratch_shapes=[pltpu.SemaphoreType.DMA((2,))],
        name="store",
    )(templates, expected)


def local(n_ev, n_sys, observables, selection, base_weight, category, bin_number, response, nuisance_pulls):
    events, features = observables.shape
    variations = response.shape[1]
    vmem = pl.BlockSpec(memory_space=pltpu.VMEM)
    hbm = pl.BlockSpec(memory_space=pltpu.HBM)
    slots = n_ev * K
    results = (
        jax.ShapeDtypeStruct((variations, B), F32),
        jax.ShapeDtypeStruct((1, B), F32),
    )
    scratch = [
        pltpu.VMEM((slots, variations), F32),
        pltpu.VMEM((slots, variations), F32),
        pltpu.VMEM((n_ev, 1, 128), F32),
        pltpu.VMEM((n_ev, 1, 128), F32),
        pltpu.VMEM((B, slots), BF16),
        pltpu.SemaphoreType.DMA,
        pltpu.SemaphoreType.DMA((ARRIVALS,)),
        pltpu.SemaphoreType.DMA,
        pltpu.SemaphoreType.DMA,
    ]
    templates, expected, most, weight, info = pl.pallas_call(
        functools.partial(exchange, n_ev, n_sys, False),
        out_shape=results + (
            jax.ShapeDtypeStruct((1, 128 - N_LANE), F32),
            jax.ShapeDtypeStruct((events, variations), F32),
            jax.ShapeDtypeStruct((8, events), F32),
        ),
        in_specs=[hbm] * 7,
        out_specs=(vmem,) * 5,
        scratch_shapes=scratch + [
            pltpu.VMEM((n_sys, 1, events), F32),
            pltpu.VMEM((1, variations // 2), F32),
            pltpu.SemaphoreType.DMA((5,)),
            pltpu.SemaphoreType.DMA((n_sys,)),
            pltpu.SemaphoreType.DMA((n_sys,)),
            pltpu.VMEM((events, features), BF16),
            pltpu.VMEM((events, features), jnp.int32),
            pltpu.VMEM((1, events), F32),
            pltpu.VMEM((1, events), jnp.int32),
            pltpu.VMEM((1, events), jnp.int32),
            pltpu.VMEM((features, variations), BF16),
            pltpu.SemaphoreType.DMA((2, STEPS)),
        ],
        compiler_params=pltpu.CompilerParams(
            collective_id=0, has_side_effects=True, vmem_limit_bytes=VMEM_BYTES
        ),
        name="first_round",
    )(
        in_hbm(observables),
        in_hbm(selection),
        in_hbm(base_weight.reshape(1, events)),
        in_hbm(category.reshape(1, events)),
        in_hbm(bin_number.reshape(1, events)),
        in_hbm(response),
        in_hbm(nuisance_pulls.reshape(1, -1)),
    )
    largest = most[0, 0].astype(jnp.int32)

    def more(carry):
        return carry[0] * K < largest

    def next_round(carry):
        index, templates, expected = carry
        extra, extra_expected = pl.pallas_call(
            functools.partial(exchange, n_ev, n_sys, True),
            out_shape=results,
            in_specs=[pl.BlockSpec(memory_space=pltpu.SMEM), vmem, vmem],
            out_specs=(vmem, vmem),
            scratch_shapes=scratch,
            compiler_params=pltpu.CompilerParams(
                collective_id=1, has_side_effects=True, vmem_limit_bytes=VMEM_BYTES
            ),
            name="later_round",
        )(index.reshape(1), weight, info)
        return index + 1, templates + extra, expected + extra_expected

    _, templates, expected = lax.while_loop(more, next_round, (jnp.int32(1), templates, expected))
    return finish(templates, expected)


def solution(mesh):
    placed = (P("ev", None), P("ev", None), P("ev"), P("ev"), P("ev"), P(None, "sys"), P("sys"))
    return jax.shard_map(
        functools.partial(local, mesh.shape["ev"], mesh.shape["sys"]),
        mesh=mesh,
        in_specs=placed,
        out_specs=(P("ev", "sys", None), P("ev", None)),
        check_vma=False,
    )
```

```python
import functools

import jax
import jax.numpy as jnp
from jax import lax
from jax.experimental import pallas as pl
from jax.experimental.pallas import tpu as pltpu
from jax.sharding import PartitionSpec as P

B = 256
K = 24
PITCH = 32
SECOND_LANE = 32
N_LANE = 64
STRIDE = 27
PACKS = 8
FIRST_PACKS = 8
ARRIVALS = 4
STEPS = 4
VMEM_BYTES = 48 << 20
MESH = pl.DeviceIdType.MESH
F32 = jnp.float32
BF16 = jnp.bfloat16


def iota(shape, dim):
    return lax.broadcasted_iota(jnp.int32, shape, dim)


def onehot(mask):
    return jnp.where(mask, 1.0, 0.0).astype(BF16)


def parts(x, count):
    out = []
    for _ in range(count):
        piece = x.astype(BF16)
        out.append(piece)
        x = x - piece.astype(F32)
    return out


def dot(a, b):
    return jnp.dot(a, b, preferred_element_type=F32)


def dot_nt(a, b):
    return lax.dot_general(a, b, (((1,), (1,)), ((), ())), preferred_element_type=F32)


def far(i):
    away = STRIDE * i % 64
    x, z, y = away // 2 % 4, away // 8 % 2, away // 16
    return -(min(x, 4 - x) + z + min(y, 4 - y))


def prepare(n_ev, me, hbm_refs, weight, info, vmem_refs, small_sem, load_sem, greet):
    obs_hbm, sel_hbm, base_hbm, cat_hbm, bin_hbm, resp_hbm = hbm_refs
    obs, sel, base_ref, cat_ref, bin_ref, resp_ref = vmem_refs
    events = obs.shape[0]
    variations = weight.shape[1]
    rows = events // STEPS

    small = []
    for i, (source, target) in enumerate((
        (cat_hbm, cat_ref), (bin_hbm, bin_ref), (base_hbm, base_ref), (resp_hbm, resp_ref),
    )):
        small.append(pltpu.make_async_copy(source, target, small_sem.at[i]))
        small[-1].start()
    loads = []
    for i in range(STEPS):
        part = pl.ds(i * rows, rows)
        loads.append((
            pltpu.make_async_copy(obs_hbm.at[part], obs.at[part], load_sem.at[0, i]),
            pltpu.make_async_copy(sel_hbm.at[part], sel.at[part], load_sem.at[1, i]),
        ))
        for load in loads[-1]:
            load.start()
    greet()

    before = onehot(iota((events, events), 0) < iota((events, events), 1))
    for copy in small:
        copy.wait()
    cat = cat_ref[...]
    away = jnp.where(cat < me, cat - me + n_ev, cat - me)
    block = away * pow(STRIDE, -1, n_ev) % n_ev
    in_block = iota((n_ev, events), 0) == block
    ahead = dot(onehot(in_block), before)
    rank = jnp.sum(jnp.where(in_block, ahead, 0.0), axis=0, keepdims=True)
    base = base_ref[...]
    info[0:1, :] = block.astype(F32)
    info[1:2, :] = rank
    info[2:3, :] = bin_ref[...].astype(F32)
    info[3:4, :] = base
    base_col = jnp.broadcast_to(base, (variations, events)).T

    for i in range(STEPS):
        part = pl.ds(i * rows, rows)
        for load in loads[i]:
            load.wait()
        masked = obs[part, :] * sel[part, :].astype(F32).astype(BF16)
        log_shift = dot(masked, resp_ref[...])
        weight[part, :] = base_col[i * rows : (i + 1) * rows] * jnp.exp(0.2 * log_shift)


def exchange(n_ev, n_sys, later, *refs):
    if later:
        (
            round_ref, weight, info, hist_ref, expected_ref,
            send, recv, terms, terms_in, picked, morph,
            send_sem, recv_sem, terms_send_sem, terms_recv_sem, morph_send_sem, morph_recv_sem,
        ) = refs
    else:
        hbm_refs, refs = refs[:6], refs[6:]
        (
            pull_hbm, hist_ref, expected_ref, most_ref, weight, info,
            send, recv, terms, terms_in, picked, morph,
            send_sem, recv_sem, terms_send_sem, terms_recv_sem, morph_send_sem, morph_recv_sem,
            share, pull_ref, small_sem, share_send_sem, share_recv_sem, *vmem_refs, load_sem,
        ) = refs
    events, variations = weight.shape
    slots = n_ev * PITCH
    me, my_sys = lax.axis_index("ev"), lax.axis_index("sys")
    barrier = pltpu.get_barrier_semaphore()

    half = n_sys // 2
    first_half = my_sys < half
    partner = n_sys - 1 - my_sys

    def to(i):
        peer = me + STRIDE * i % n_ev
        return {"ev": jnp.where(peer >= n_ev, peer - n_ev, peer)}

    def greet():
        if later:
            @pl.when(my_sys >= half)
            def _():
                pl.semaphore_signal(barrier, inc=1, device_id={"sys": partner}, device_id_type=MESH)
        else:
            for q in range(n_sys):
                @pl.when(jnp.logical_and(q != my_sys, jnp.logical_or(first_half, q >= half)))
                def _():
                    pl.semaphore_signal(barrier, inc=1, device_id={"sys": q}, device_id_type=MESH)

        for i in sorted(range(1, n_ev), key=far):
            pl.semaphore_signal(barrier, inc=1, device_id=to(i), device_id_type=MESH)

    def share_copy(sender, target):
        return pltpu.make_async_remote_copy(
            src_ref=share.at[my_sys],
            dst_ref=share.at[my_sys],
            send_sem=share_send_sem.at[target],
            recv_sem=share_recv_sem.at[sender],
            device_id={"sys": target},
            device_id_type=MESH,
        )

    recv[:, K:, :] = jnp.zeros((n_ev, PITCH - K, variations), F32)
    if later:
        greet()
        pl.semaphore_wait(barrier, n_ev - 1 + jnp.where(first_half, 1, 0))
    else:
        pull_copy = pltpu.make_async_copy(pull_hbm, pull_ref, small_sem.at[4])
        pull_copy.start()
        @pl.when(my_sys >= half)
        def _():
            share[0:half] = jnp.zeros((half, 1, events), F32)

        prepare(n_ev, me, hbm_refs, weight, info, vmem_refs, small_sem, load_sem, greet)

        pull_copy.wait()
        var_at = iota((variations, variations // 2), 0)
        mine = iota((variations, variations // 2), 1) == var_at // 2
        pull = jnp.sum(jnp.where(mine, pull_ref[...], 0.0), axis=1, keepdims=True)
        odd = iota((variations, 1), 0) % 2
        coef = jnp.maximum(jnp.where(odd == 0, pull, -pull), 0.0)
        share[my_sys] = jnp.sum(coef * (weight[...].T - info[3:4, :]), axis=0, keepdims=True)
        pl.semaphore_wait(barrier, n_ev - 1 + jnp.where(first_half, half - 1, n_sys - 1))
        for q in range(n_sys):
            @pl.when(jnp.logical_and(q != my_sys, jnp.logical_or(my_sys >= half, q < half)))
            def _():
                share_copy(my_sys, q).start()

    block = info[0:1, :].astype(jnp.int32)
    rank_f = info[1:2, :]
    most = jnp.max(rank_f, axis=1, keepdims=True) + 1.0
    rank = rank_f.astype(jnp.int32)
    if later:
        rank = rank - round_ref[0] * K
    kept = jnp.logical_and(rank >= 0, rank < K)
    slot = jnp.where(kept, block * PITCH + rank, -1)
    rank = jnp.where(kept, rank, -1)
    in_block = iota((n_ev, events), 0) == block
    at_place = onehot(iota((128, events), 0) == rank)
    tags = dot_nt(jnp.where(in_block, info[2:3, :], 0.0).astype(BF16), at_place)
    tags = jnp.where(iota(tags.shape, 1) >= N_LANE, most, tags)

    halves = jnp.concatenate(parts(weight[...], 2), axis=1)
    blocks = n_ev // PACKS
    count = blocks * PITCH

    def pack(p):
        pick = onehot(iota((count, events), 0) + p * count == slot)
        both = dot(pick, halves)
        both = (both[:, :variations] + both[:, variations:]).reshape(blocks, PITCH, variations)
        tag = tags[p * blocks : (p + 1) * blocks, None, :]
        send[pl.ds(p * blocks, blocks)] = jnp.where(iota(both.shape, 1) == K, tag, both)
        for i in range(p * blocks, (p + 1) * blocks):
            if i > 0:
                pltpu.make_async_remote_copy(
                    src_ref=send.at[i, pl.ds(0, K + 1)],
                    dst_ref=recv.at[i, pl.ds(0, K + 1)],
                    send_sem=send_sem,
                    recv_sem=recv_sem.at[i * ARRIVALS // n_ev],
                    device_id=to(i),
                    device_id_type=MESH,
                ).start()

    for p in range(FIRST_PACKS):
        pack(p)
    recv[0, :, :] = send[0, :, :]

    if not later:
        for q in range(n_sys):
            @pl.when(jnp.logical_and(q != my_sys, jnp.logical_or(first_half, q >= half)))
            def _():
                share_copy(q, q).wait_recv()

        info[3:4, :] = info[3:4, :] + sum(share[q] for q in range(1, half)) + share[0]
        info[4:5, :] = sum(share[q] for q in range(half + 1, n_sys)) + share[half]
    pieces = parts(info[3:4, :], 2) + parts(info[4:5, :], 2)
    stacked = [jnp.where(in_block, piece.astype(F32), 0.0).astype(BF16) for piece in pieces]
    row = dot_nt(jnp.concatenate(stacked, axis=0), at_place)
    row = (
        row[:n_ev] + row[n_ev : 2 * n_ev]
        + pltpu.roll(row[2 * n_ev : 3 * n_ev] + row[3 * n_ev :], SECOND_LANE, axis=1)
    )
    terms[...] = row[:, None, :]

    def terms_copy(blocks, peer):
        return pltpu.make_async_remote_copy(
            src_ref=terms.at[blocks], dst_ref=terms_in.at[blocks], send_sem=terms_send_sem,
            recv_sem=terms_recv_sem, device_id=to(peer), device_id_type=MESH,
        )

    for i in range(1, n_ev):
        terms_copy(i, i).start()
    terms_in[0] = terms[0]
    for p in range(FIRST_PACKS, PACKS):
        pack(p)

    blocks = n_ev // ARRIVALS
    count = blocks * PITCH
    at = iota((1, count), 1)
    place = at % PITCH
    used = place < K
    ours = iota((blocks, count), 0) == at // PITCH
    spread = onehot(jnp.logical_and(iota((128, count), 0) == place, used))

    def flat(rows):
        spaced = dot(rows, spread).reshape(-1, blocks, count)
        return jnp.sum(jnp.where(ours[None], spaced, 0.0), axis=1)

    def arrived(a):
        first = a * blocks
        some = pl.ds(max(first, 1), first + blocks - max(first, 1))
        pltpu.make_async_remote_copy(
            src_ref=send.at[some, pl.ds(0, K + 1)], dst_ref=recv.at[some, pl.ds(0, K + 1)],
            send_sem=send_sem, recv_sem=recv_sem.at[a], device_id=to(1), device_id_type=MESH,
        ).wait_recv()
        tag = recv[pl.ds(first, blocks), K, :]
        bins = jnp.where(used, flat(tag.astype(BF16)), -1.0).astype(jnp.int32)
        in_bin = onehot(iota((B, count), 0) == bins)
        picked[:, a * count : (a + 1) * count] = in_bin
        rows = recv[pl.ds(first, blocks)].reshape(count, variations)
        return dot(in_bin, jnp.concatenate(parts(rows, 2), axis=1)), jnp.max(tag[:, N_LANE:], axis=0, keepdims=True)

    total, most = arrived(0)
    for a in range(1, ARRIVALS):
        more_total, more_most = arrived(a)
        total, most = total + more_total, jnp.maximum(most, more_most)
    hist_ref[...] = (total[:, :variations] + total[:, variations:]).T
    if not later:
        most_ref[...] = most

    terms_copy(pl.ds(1, n_ev - 1), 1).wait()
    got = terms_in[:, 0, :]
    pieces = parts(got, 2) + parts(pltpu.roll(got, 128 - SECOND_LANE, axis=1), 2)
    lanes = [
        flat(jnp.concatenate([piece[a * blocks : (a + 1) * blocks] for piece in pieces], axis=0))
        for a in range(ARRIVALS)
    ]
    lanes = jnp.concatenate([jnp.concatenate(lanes, axis=1), jnp.zeros((4, slots), F32)], axis=0)
    morphed = dot_nt(lanes.astype(BF16), picked[...])
    morph_copy = pltpu.make_async_remote_copy(
        src_ref=morph, dst_ref=morph, send_sem=morph_send_sem, recv_sem=morph_recv_sem,
        device_id={"sys": partner}, device_id_type=MESH,
    )

    @pl.when(first_half)
    def _():
        morph[...] = morphed[0:1] + morphed[1:2]
        morph_copy.start()

    @pl.when(my_sys >= half)
    def _():
        morph_copy.wait_recv()

    expected_ref[...] = morph[...] + (morphed[2:3] + morphed[3:4])

    sent = pl.ds(1, n_ev - 1)
    pltpu.make_async_remote_copy(
        src_ref=send.at[sent, pl.ds(0, K + 1)], dst_ref=recv.at[sent, pl.ds(0, K + 1)],
        send_sem=send_sem, recv_sem=recv_sem.at[0], device_id=to(1), device_id_type=MESH,
    ).wait_send()
    @pl.when(first_half)
    def _():
        morph_copy.wait_send()

    if not later:
        for q in range(n_sys):
            @pl.when(jnp.logical_and(q != my_sys, jnp.logical_or(my_sys >= half, q < half)))
            def _():
                share_copy(my_sys, q).wait_send()


def in_hbm(x):
    return pltpu.with_memory_space_constraint(x, pltpu.HBM)


def store(hist_ref, expected_ref, templates_hbm, expected_hbm, sem):
    copies = (
        pltpu.make_async_copy(hist_ref, templates_hbm.at[0], sem.at[0]),
        pltpu.make_async_copy(expected_ref, expected_hbm, sem.at[1]),
    )
    for copy in copies:
        copy.start()
    for copy in copies:
        copy.wait()


def finish(templates, expected):
    vmem = pl.BlockSpec(memory_space=pltpu.VMEM)
    hbm = pl.BlockSpec(memory_space=pltpu.HBM)
    return pl.pallas_call(
        store,
        out_shape=(
            jax.ShapeDtypeStruct((1,) + templates.shape, F32),
            jax.ShapeDtypeStruct(expected.shape, F32),
        ),
        in_specs=[vmem] * 2,
        out_specs=(hbm, hbm),
        scratch_shapes=[pltpu.SemaphoreType.DMA((2,))],
        name="store",
    )(templates, expected)


def local(n_ev, n_sys, observables, selection, base_weight, category, bin_number, response, nuisance_pulls):
    events, features = observables.shape
    variations = response.shape[1]
    vmem = pl.BlockSpec(memory_space=pltpu.VMEM)
    hbm = pl.BlockSpec(memory_space=pltpu.HBM)
    slots = n_ev * PITCH
    results = (
        jax.ShapeDtypeStruct((variations, B), F32),
        jax.ShapeDtypeStruct((1, B), F32),
    )
    scratch = [
        pltpu.VMEM((n_ev, PITCH, variations), F32),
        pltpu.VMEM((n_ev, PITCH, variations), F32),
        pltpu.VMEM((n_ev, 1, 128), F32),
        pltpu.VMEM((n_ev, 1, 128), F32),
        pltpu.VMEM((B, slots), BF16),
        pltpu.VMEM((1, B), F32),
        pltpu.SemaphoreType.DMA,
        pltpu.SemaphoreType.DMA((ARRIVALS,)),
        pltpu.SemaphoreType.DMA,
        pltpu.SemaphoreType.DMA,
        pltpu.SemaphoreType.DMA,
        pltpu.SemaphoreType.DMA,
    ]
    templates, expected, most, weight, info = pl.pallas_call(
        functools.partial(exchange, n_ev, n_sys, False),
        out_shape=results + (
            jax.ShapeDtypeStruct((1, 128 - N_LANE), F32),
            jax.ShapeDtypeStruct((events, variations), F32),
            jax.ShapeDtypeStruct((8, events), F32),
        ),
        in_specs=[hbm] * 7,
        out_specs=(vmem,) * 5,
        scratch_shapes=scratch + [
            pltpu.VMEM((n_sys, 1, events), F32),
            pltpu.VMEM((1, variations // 2), F32),
            pltpu.SemaphoreType.DMA((5,)),
            pltpu.SemaphoreType.DMA((n_sys,)),
            pltpu.SemaphoreType.DMA((n_sys,)),
            pltpu.VMEM((events, features), BF16),
            pltpu.VMEM((events, features), jnp.int32),
            pltpu.VMEM((1, events), F32),
            pltpu.VMEM((1, events), jnp.int32),
            pltpu.VMEM((1, events), jnp.int32),
            pltpu.VMEM((features, variations), BF16),
            pltpu.SemaphoreType.DMA((2, STEPS)),
        ],
        compiler_params=pltpu.CompilerParams(
            collective_id=0, has_side_effects=True, vmem_limit_bytes=VMEM_BYTES
        ),
        name="first_round",
    )(
        in_hbm(observables),
        in_hbm(selection),
        in_hbm(base_weight.reshape(1, events)),
        in_hbm(category.reshape(1, events)),
        in_hbm(bin_number.reshape(1, events)),
        in_hbm(response),
        in_hbm(nuisance_pulls.reshape(1, -1)),
    )
    largest = most[0, 0].astype(jnp.int32)

    def more(carry):
        return carry[0] * K < largest

    def next_round(carry):
        index, templates, expected = carry
        extra, extra_expected = pl.pallas_call(
            functools.partial(exchange, n_ev, n_sys, True),
            out_shape=results,
            in_specs=[pl.BlockSpec(memory_space=pltpu.SMEM), vmem, vmem],
            out_specs=(vmem, vmem),
            scratch_shapes=scratch,
            compiler_params=pltpu.CompilerParams(
                collective_id=1, has_side_effects=True, vmem_limit_bytes=VMEM_BYTES
            ),
            name="later_round",
        )(index.reshape(1), weight, info)
        return index + 1, templates + extra, expected + extra_expected

    _, templates, expected = lax.while_loop(more, next_round, (jnp.int32(1), templates, expected))
    return finish(templates, expected)


def solution(mesh):
    placed = (P("ev", None), P("ev", None), P("ev"), P("ev"), P("ev"), P(None, "sys"), P("sys"))
    return jax.shard_map(
        functools.partial(local, mesh.shape["ev"], mesh.shape["sys"]),
        mesh=mesh,
        in_specs=placed,
        out_specs=(P("ev", "sys", None), P("ev", None)),
        check_vma=False,
    )
```

```python
import functools

import jax
import jax.numpy as jnp
from jax import lax
from jax.experimental import pallas as pl
from jax.experimental.pallas import tpu as pltpu
from jax.sharding import PartitionSpec as P

B = 256
K = 24
PITCH = 32
SECOND_LANE = 32
N_LANE = 64
PACKS = 8
FIRST_PACKS = 7
ARRIVALS = 4
STEPS = 4
VMEM_BYTES = 48 << 20
MESH = pl.DeviceIdType.MESH
F32 = jnp.float32
BF16 = jnp.bfloat16


def iota(shape, dim):
    return lax.broadcasted_iota(jnp.int32, shape, dim)


def onehot(mask):
    return jnp.where(mask, 1.0, 0.0).astype(BF16)


def parts(x, count):
    out = []
    for _ in range(count):
        piece = x.astype(BF16)
        out.append(piece)
        x = x - piece.astype(F32)
    return out


def dot(a, b):
    return jnp.dot(a, b, preferred_element_type=F32)


def dot_nt(a, b):
    return lax.dot_general(a, b, (((1,), (1,)), ((), ())), preferred_element_type=F32)


SIZES = (2, 4, 2, 4)
PLACES = sorted(range(64), key=lambda d: (d != 0, -sum(min(e, n - e) for e, n in zip(
    (d // 2 % 4, d // 8 % 2, d // 16), (4, 2, 4))), d % 2, d * 27 % 64))


def digits(position):
    out = []
    for size in SIZES:
        out.append(position % size)
        position = position // size
    return out


def prepare(n_ev, me, hbm_refs, weight, info, vmem_refs, small_sem, load_sem, greet):
    obs_hbm, sel_hbm, base_hbm, cat_hbm, bin_hbm, resp_hbm = hbm_refs
    obs, sel, base_ref, cat_ref, bin_ref, resp_ref = vmem_refs
    events = obs.shape[0]
    variations = weight.shape[1]
    rows = events // STEPS

    small = []
    for i, (source, target) in enumerate((
        (cat_hbm, cat_ref), (bin_hbm, bin_ref), (base_hbm, base_ref), (resp_hbm, resp_ref),
    )):
        small.append(pltpu.make_async_copy(source, target, small_sem.at[i]))
        small[-1].start()
    loads = []
    for i in range(STEPS):
        part = pl.ds(i * rows, rows)
        loads.append((
            pltpu.make_async_copy(obs_hbm.at[part], obs.at[part], load_sem.at[0, i]),
            pltpu.make_async_copy(sel_hbm.at[part], sel.at[part], load_sem.at[1, i]),
        ))
        for load in loads[-1]:
            load.start()
    greet()

    before = onehot(iota((events, events), 0) < iota((events, events), 1))
    for copy in small:
        copy.wait()
    cat = cat_ref[...]
    away, stride = 0, 1
    for digit, own, size in zip(digits(cat), digits(me), SIZES):
        away = away + (digit - own + size) % size * stride
        stride = stride * size
    at = iota((8, n_ev), 1)
    order = sum(jnp.where(at == place, i, 0) for i, place in enumerate(PLACES))
    block = dot(order.astype(F32).astype(BF16), onehot(iota((n_ev, events), 0) == away))[0:1].astype(jnp.int32)
    in_block = iota((n_ev, events), 0) == block
    ahead = dot(onehot(in_block), before)
    rank = jnp.sum(jnp.where(in_block, ahead, 0.0), axis=0, keepdims=True)
    base = base_ref[...]
    info[0:1, :] = block.astype(F32)
    info[1:2, :] = rank
    info[2:3, :] = bin_ref[...].astype(F32)
    info[3:4, :] = base
    return loads


def weigh(loads, weight, info, obs, sel, resp_ref):
    events, variations = weight.shape
    rows = events // STEPS
    base_col = jnp.broadcast_to(info[3:4, :], (variations, events)).T
    for i in range(STEPS):
        part = pl.ds(i * rows, rows)
        for load in loads[i]:
            load.wait()
        masked = obs[part, :] * sel[part, :].astype(F32).astype(BF16)
        log_shift = dot(masked, resp_ref[...])
        weight[part, :] = base_col[i * rows : (i + 1) * rows] * jnp.exp(0.2 * log_shift)


def exchange(n_ev, n_sys, later, *refs):
    if later:
        (
            round_ref, weight, info, hist_ref, expected_ref,
            send, recv, terms, terms_in, picked, morph,
            send_sem, recv_sem, terms_send_sem, terms_recv_sem, morph_send_sem, morph_recv_sem,
        ) = refs
    else:
        hbm_refs, refs = refs[:6], refs[6:]
        (
            pull_hbm, hist_ref, expected_ref, most_ref, weight, info,
            send, recv, terms, terms_in, picked, morph,
            send_sem, recv_sem, terms_send_sem, terms_recv_sem, morph_send_sem, morph_recv_sem,
            share, pull_ref, small_sem, share_send_sem, share_recv_sem, *vmem_refs, load_sem,
        ) = refs
    events, variations = weight.shape
    slots = n_ev * PITCH
    me, my_sys = lax.axis_index("ev"), lax.axis_index("sys")
    barrier = pltpu.get_barrier_semaphore()

    half = n_sys // 2
    first_half = my_sys < half
    partner = n_sys - 1 - my_sys

    shifted, stride = [], 1
    for own, size in zip(digits(me), SIZES):
        shifted.append([lax.rem(own + e, size) * stride for e in range(size)])
        stride = stride * size

    def to(i):
        return {"ev": sum(values[e] for values, e in zip(shifted, digits(PLACES[i])))}

    def greet():
        if later:
            @pl.when(my_sys >= half)
            def _():
                pl.semaphore_signal(barrier, inc=1, device_id={"sys": partner}, device_id_type=MESH)
        else:
            for q in range(n_sys):
                @pl.when(jnp.logical_and(q != my_sys, jnp.logical_or(first_half, q >= half)))
                def _():
                    pl.semaphore_signal(barrier, inc=1, device_id={"sys": q}, device_id_type=MESH)

        for i in range(1, n_ev):
            pl.semaphore_signal(barrier, inc=1, device_id=to(i), device_id_type=MESH)

    def share_copy(sender, target):
        return pltpu.make_async_remote_copy(
            src_ref=share.at[my_sys],
            dst_ref=share.at[my_sys],
            send_sem=share_send_sem.at[target],
            recv_sem=share_recv_sem.at[sender],
            device_id={"sys": target},
            device_id_type=MESH,
        )

    recv[:, K:, :] = jnp.zeros((n_ev, PITCH - K, variations), F32)
    if later:
        greet()
    else:
        pull_copy = pltpu.make_async_copy(pull_hbm, pull_ref, small_sem.at[4])
        pull_copy.start()

        @pl.when(my_sys >= half)
        def _():
            share[0:half] = jnp.zeros((half, 1, events), F32)

        loads = prepare(n_ev, me, hbm_refs, weight, info, vmem_refs, small_sem, load_sem, greet)

    block = info[0:1, :].astype(jnp.int32)
    rank_f = info[1:2, :]
    most = jnp.max(rank_f, axis=1, keepdims=True) + 1.0
    rank = rank_f.astype(jnp.int32)
    if later:
        rank = rank - round_ref[0] * K
    kept = jnp.logical_and(rank >= 0, rank < K)
    slot = jnp.where(kept, block * PITCH + rank, -1)
    rank = jnp.where(kept, rank, -1)
    in_block = iota((n_ev, events), 0) == block
    at_place = onehot(iota((128, events), 0) == rank)
    tags = dot_nt(jnp.where(in_block, info[2:3, :], 0.0).astype(BF16), at_place)
    tags = jnp.where(iota(tags.shape, 1) >= N_LANE, most, tags)

    if not later:
        weigh(loads, weight, info, vmem_refs[0], vmem_refs[1], vmem_refs[5])

        pull_copy.wait()
        var_at = iota((variations, variations // 2), 0)
        mine = iota((variations, variations // 2), 1) == var_at // 2
        pull = jnp.sum(jnp.where(mine, pull_ref[...], 0.0), axis=1, keepdims=True)
        odd = iota((variations, 1), 0) % 2
        coef = jnp.maximum(jnp.where(odd == 0, pull, -pull), 0.0)
        share[my_sys] = jnp.sum(coef * (weight[...].T - info[3:4, :]), axis=0, keepdims=True)

    halves = jnp.concatenate(parts(weight[...], 2), axis=1)
    blocks = n_ev // PACKS
    count = blocks * PITCH

    def fill(p):
        pick = onehot(iota((count, events), 0) + p * count == slot)
        both = dot(pick, halves)
        both = (both[:, :variations] + both[:, variations:]).reshape(blocks, PITCH, variations)
        tag = tags[p * blocks : (p + 1) * blocks, None, :]
        send[pl.ds(p * blocks, blocks)] = jnp.where(iota(both.shape, 1) == K, tag, both)

    def ship(p):
        for i in range(p * blocks, (p + 1) * blocks):
            if i > 0:
                pltpu.make_async_remote_copy(
                    src_ref=send.at[i, pl.ds(0, K + 1)],
                    dst_ref=recv.at[i, pl.ds(0, K + 1)],
                    send_sem=send_sem,
                    recv_sem=recv_sem.at[i * ARRIVALS // n_ev],
                    device_id=to(i),
                    device_id_type=MESH,
                ).start()

    if later:
        pl.semaphore_wait(barrier, n_ev - 1 + jnp.where(first_half, 1, 0))
    else:
        pl.semaphore_wait(barrier, n_ev - 1 + jnp.where(first_half, half - 1, n_sys - 1))
        for q in range(n_sys):
            @pl.when(jnp.logical_and(q != my_sys, jnp.logical_or(my_sys >= half, q < half)))
            def _():
                share_copy(my_sys, q).start()

    fill(0)
    ship(0)
    for p in range(1, FIRST_PACKS):
        fill(p)
        ship(p)
    recv[0, :, :] = send[0, :, :]

    if not later:
        for q in range(n_sys):
            @pl.when(jnp.logical_and(q != my_sys, jnp.logical_or(first_half, q >= half)))
            def _():
                share_copy(q, q).wait_recv()

        info[3:4, :] = info[3:4, :] + sum(share[q] for q in range(1, half)) + share[0]
        info[4:5, :] = sum(share[q] for q in range(half + 1, n_sys)) + share[half]
    pieces = parts(info[3:4, :], 2) + parts(info[4:5, :], 2)
    stacked = [jnp.where(in_block, piece.astype(F32), 0.0).astype(BF16) for piece in pieces]
    row = dot_nt(jnp.concatenate(stacked, axis=0), at_place)
    row = (
        row[:n_ev] + row[n_ev : 2 * n_ev]
        + pltpu.roll(row[2 * n_ev : 3 * n_ev] + row[3 * n_ev :], SECOND_LANE, axis=1)
    )
    terms[...] = row[:, None, :]

    def terms_copy(blocks, peer):
        return pltpu.make_async_remote_copy(
            src_ref=terms.at[blocks], dst_ref=terms_in.at[blocks], send_sem=terms_send_sem,
            recv_sem=terms_recv_sem, device_id=to(peer), device_id_type=MESH,
        )

    for i in range(1, n_ev):
        terms_copy(i, i).start()
    terms_in[0] = terms[0]
    for p in range(FIRST_PACKS, PACKS):
        fill(p)
        ship(p)

    blocks = n_ev // ARRIVALS
    count = blocks * PITCH
    at = iota((1, count), 1)
    place = at % PITCH
    used = place < K
    ours = iota((blocks, count), 0) == at // PITCH
    spread = onehot(jnp.logical_and(iota((128, count), 0) == place, used))

    def flat(rows):
        spaced = dot(rows, spread).reshape(-1, blocks, count)
        return jnp.sum(jnp.where(ours[None], spaced, 0.0), axis=1)

    def arrived(a):
        first = a * blocks
        some = pl.ds(max(first, 1), first + blocks - max(first, 1))
        pltpu.make_async_remote_copy(
            src_ref=send.at[some, pl.ds(0, K + 1)], dst_ref=recv.at[some, pl.ds(0, K + 1)],
            send_sem=send_sem, recv_sem=recv_sem.at[a], device_id=to(1), device_id_type=MESH,
        ).wait_recv()
        tag = recv[pl.ds(first, blocks), K, :]
        bins = jnp.where(used, flat(tag.astype(BF16)), -1.0).astype(jnp.int32)
        in_bin = onehot(iota((B, count), 0) == bins)
        picked[:, a * count : (a + 1) * count] = in_bin
        rows = recv[pl.ds(first, blocks)].reshape(count, variations)
        return dot(in_bin, jnp.concatenate(parts(rows, 2), axis=1)), jnp.max(tag[:, N_LANE:], axis=0, keepdims=True)

    total, most = arrived(0)
    for a in range(1, ARRIVALS):
        more_total, more_most = arrived(a)
        total, most = total + more_total, jnp.maximum(most, more_most)
    hist_ref[...] = (total[:, :variations] + total[:, variations:]).T
    if not later:
        most_ref[...] = most

    terms_copy(pl.ds(1, n_ev - 1), 1).wait()
    got = terms_in[:, 0, :]
    pieces = parts(got, 2) + parts(pltpu.roll(got, 128 - SECOND_LANE, axis=1), 2)
    lanes = [
        flat(jnp.concatenate([piece[a * blocks : (a + 1) * blocks] for piece in pieces], axis=0))
        for a in range(ARRIVALS)
    ]
    lanes = jnp.concatenate([jnp.concatenate(lanes, axis=1), jnp.zeros((4, slots), F32)], axis=0)
    morphed = dot_nt(lanes.astype(BF16), picked[...])
    morph_copy = pltpu.make_async_remote_copy(
        src_ref=morph, dst_ref=morph, send_sem=morph_send_sem, recv_sem=morph_recv_sem,
        device_id={"sys": partner}, device_id_type=MESH,
    )

    @pl.when(first_half)
    def _():
        morph[...] = morphed[0:1] + morphed[1:2]
        morph_copy.start()

    @pl.when(my_sys >= half)
    def _():
        morph_copy.wait_recv()

    expected_ref[...] = morph[...] + (morphed[2:3] + morphed[3:4])

    sent = pl.ds(1, n_ev - 1)
    pltpu.make_async_remote_copy(
        src_ref=send.at[sent, pl.ds(0, K + 1)], dst_ref=recv.at[sent, pl.ds(0, K + 1)],
        send_sem=send_sem, recv_sem=recv_sem.at[0], device_id=to(1), device_id_type=MESH,
    ).wait_send()
    @pl.when(first_half)
    def _():
        morph_copy.wait_send()

    if not later:
        for q in range(n_sys):
            @pl.when(jnp.logical_and(q != my_sys, jnp.logical_or(my_sys >= half, q < half)))
            def _():
                share_copy(my_sys, q).wait_send()


def in_hbm(x):
    return pltpu.with_memory_space_constraint(x, pltpu.HBM)


def store(hist_ref, expected_ref, templates_hbm, expected_hbm, sem):
    copies = (
        pltpu.make_async_copy(hist_ref, templates_hbm.at[0], sem.at[0]),
        pltpu.make_async_copy(expected_ref, expected_hbm, sem.at[1]),
    )
    for copy in copies:
        copy.start()
    for copy in copies:
        copy.wait()


def finish(templates, expected):
    vmem = pl.BlockSpec(memory_space=pltpu.VMEM)
    hbm = pl.BlockSpec(memory_space=pltpu.HBM)
    return pl.pallas_call(
        store,
        out_shape=(
            jax.ShapeDtypeStruct((1,) + templates.shape, F32),
            jax.ShapeDtypeStruct(expected.shape, F32),
        ),
        in_specs=[vmem] * 2,
        out_specs=(hbm, hbm),
        scratch_shapes=[pltpu.SemaphoreType.DMA((2,))],
        name="store",
    )(templates, expected)


def local(n_ev, n_sys, observables, selection, base_weight, category, bin_number, response, nuisance_pulls):
    events, features = observables.shape
    variations = response.shape[1]
    vmem = pl.BlockSpec(memory_space=pltpu.VMEM)
    hbm = pl.BlockSpec(memory_space=pltpu.HBM)
    slots = n_ev * PITCH
    results = (
        jax.ShapeDtypeStruct((variations, B), F32),
        jax.ShapeDtypeStruct((1, B), F32),
    )
    scratch = [
        pltpu.VMEM((n_ev, PITCH, variations), F32),
        pltpu.VMEM((n_ev, PITCH, variations), F32),
        pltpu.VMEM((n_ev, 1, 128), F32),
        pltpu.VMEM((n_ev, 1, 128), F32),
        pltpu.VMEM((B, slots), BF16),
        pltpu.VMEM((1, B), F32),
        pltpu.SemaphoreType.DMA,
        pltpu.SemaphoreType.DMA((ARRIVALS,)),
        pltpu.SemaphoreType.DMA,
        pltpu.SemaphoreType.DMA,
        pltpu.SemaphoreType.DMA,
        pltpu.SemaphoreType.DMA,
    ]
    templates, expected, most, weight, info = pl.pallas_call(
        functools.partial(exchange, n_ev, n_sys, False),
        out_shape=results + (
            jax.ShapeDtypeStruct((1, 128 - N_LANE), F32),
            jax.ShapeDtypeStruct((events, variations), F32),
            jax.ShapeDtypeStruct((8, events), F32),
        ),
        in_specs=[hbm] * 7,
        out_specs=(vmem,) * 5,
        scratch_shapes=scratch + [
            pltpu.VMEM((n_sys, 1, events), F32),
            pltpu.VMEM((1, variations // 2), F32),
            pltpu.SemaphoreType.DMA((5,)),
            pltpu.SemaphoreType.DMA((n_sys,)),
            pltpu.SemaphoreType.DMA((n_sys,)),
            pltpu.VMEM((events, features), BF16),
            pltpu.VMEM((events, features), jnp.int32),
            pltpu.VMEM((1, events), F32),
            pltpu.VMEM((1, events), jnp.int32),
            pltpu.VMEM((1, events), jnp.int32),
            pltpu.VMEM((features, variations), BF16),
            pltpu.SemaphoreType.DMA((2, STEPS)),
        ],
        compiler_params=pltpu.CompilerParams(
            collective_id=0, has_side_effects=True, vmem_limit_bytes=VMEM_BYTES
        ),
        name="first_round",
    )(
        in_hbm(observables),
        in_hbm(selection),
        in_hbm(base_weight.reshape(1, events)),
        in_hbm(category.reshape(1, events)),
        in_hbm(bin_number.reshape(1, events)),
        in_hbm(response),
        in_hbm(nuisance_pulls.reshape(1, -1)),
    )
    largest = most[0, 0].astype(jnp.int32)

    def more(carry):
        return carry[0] * K < largest

    def next_round(carry):
        index, templates, expected = carry
        extra, extra_expected = pl.pallas_call(
            functools.partial(exchange, n_ev, n_sys, True),
            out_shape=results,
            in_specs=[pl.BlockSpec(memory_space=pltpu.SMEM), vmem, vmem],
            out_specs=(vmem, vmem),
            scratch_shapes=scratch,
            compiler_params=pltpu.CompilerParams(
                collective_id=1, has_side_effects=True, vmem_limit_bytes=VMEM_BYTES
            ),
            name="later_round",
        )(index.reshape(1), weight, info)
        return index + 1, templates + extra, expected + extra_expected

    _, templates, expected = lax.while_loop(more, next_round, (jnp.int32(1), templates, expected))
    return finish(templates, expected)


def solution(mesh):
    placed = (P("ev", None), P("ev", None), P("ev"), P("ev"), P("ev"), P(None, "sys"), P("sys"))
    return jax.shard_map(
        functools.partial(local, mesh.shape["ev"], mesh.shape["sys"]),
        mesh=mesh,
        in_specs=placed,
        out_specs=(P("ev", "sys", None), P("ev", None)),
        check_vma=False,
    )
```

```python
import functools

import jax
import jax.numpy as jnp
from jax import lax
from jax.experimental import pallas as pl
from jax.experimental.pallas import tpu as pltpu
from jax.sharding import PartitionSpec as P

B = 256
K = 24
PITCH = 32
SECOND_LANE = 32
N_LANE = 64
PACKS = 8
FIRST_PACKS = 7
ARRIVALS = 8
STEPS = 4
VMEM_BYTES = 48 << 20
MESH = pl.DeviceIdType.MESH
F32 = jnp.float32
BF16 = jnp.bfloat16


def iota(shape, dim):
    return lax.broadcasted_iota(jnp.int32, shape, dim)


def onehot(mask):
    return jnp.where(mask, 1.0, 0.0).astype(BF16)


def parts(x, count):
    out = []
    for _ in range(count):
        piece = x.astype(BF16)
        out.append(piece)
        x = x - piece.astype(F32)
    return out


def dot(a, b):
    return jnp.dot(a, b, preferred_element_type=F32)


def dot_nt(a, b):
    return lax.dot_general(a, b, (((1,), (1,)), ((), ())), preferred_element_type=F32)


SIZES = (2, 4, 2, 4)
PLACES = sorted(range(64), key=lambda d: (d != 0, -sum(min(e, n - e) for e, n in zip(
    (d // 2 % 4, d // 8 % 2, d // 16), (4, 2, 4))), d % 2, d * 27 % 64))


def digits(position):
    out = []
    for size in SIZES:
        out.append(position % size)
        position = position // size
    return out


def prepare(n_ev, me, hbm_refs, weight, info, vmem_refs, small_sem, load_sem, greet):
    obs_hbm, sel_hbm, base_hbm, cat_hbm, bin_hbm, resp_hbm = hbm_refs
    obs, sel, base_ref, cat_ref, bin_ref, resp_ref = vmem_refs
    events = obs.shape[0]
    variations = weight.shape[1]
    rows = events // STEPS

    small = []
    for i, (source, target) in enumerate((
        (cat_hbm, cat_ref), (bin_hbm, bin_ref), (base_hbm, base_ref), (resp_hbm, resp_ref),
    )):
        small.append(pltpu.make_async_copy(source, target, small_sem.at[i]))
        small[-1].start()
    loads = []
    for i in range(STEPS):
        part = pl.ds(i * rows, rows)
        loads.append((
            pltpu.make_async_copy(obs_hbm.at[part], obs.at[part], load_sem.at[0, i]),
            pltpu.make_async_copy(sel_hbm.at[part], sel.at[part], load_sem.at[1, i]),
        ))
        for load in loads[-1]:
            load.start()
    greet()

    before = onehot(iota((events, events), 0) < iota((events, events), 1))
    for copy in small:
        copy.wait()
    cat = cat_ref[...]
    away, stride = 0, 1
    for digit, own, size in zip(digits(cat), digits(me), SIZES):
        away = away + (digit - own + size) % size * stride
        stride = stride * size
    at = iota((8, n_ev), 1)
    order = sum(jnp.where(at == place, i, 0) for i, place in enumerate(PLACES))
    block = dot(order.astype(F32).astype(BF16), onehot(iota((n_ev, events), 0) == away))[0:1].astype(jnp.int32)
    in_block = iota((n_ev, events), 0) == block
    ahead = dot(onehot(in_block), before)
    rank = jnp.sum(jnp.where(in_block, ahead, 0.0), axis=0, keepdims=True)
    base = base_ref[...]
    info[0:1, :] = block.astype(F32)
    info[1:2, :] = rank
    info[2:3, :] = bin_ref[...].astype(F32)
    info[3:4, :] = base
    return loads


def weigh(loads, weight, info, obs, sel, resp_ref):
    events, variations = weight.shape
    rows = events // STEPS
    base_col = jnp.broadcast_to(info[3:4, :], (variations, events)).T
    for i in range(STEPS):
        part = pl.ds(i * rows, rows)
        for load in loads[i]:
            load.wait()
        masked = obs[part, :] * sel[part, :].astype(F32).astype(BF16)
        log_shift = dot(masked, resp_ref[...])
        weight[part, :] = base_col[i * rows : (i + 1) * rows] * jnp.exp(0.2 * log_shift)


def exchange(n_ev, n_sys, later, *refs):
    if later:
        (
            round_ref, weight, info, hist_ref, expected_ref,
            send, recv, terms, terms_in, picked, morph,
            send_sem, recv_sem, terms_send_sem, terms_recv_sem, morph_send_sem, morph_recv_sem,
        ) = refs
    else:
        hbm_refs, refs = refs[:6], refs[6:]
        (
            pull_hbm, hist_ref, expected_ref, most_ref, weight, info,
            send, recv, terms, terms_in, picked, morph,
            send_sem, recv_sem, terms_send_sem, terms_recv_sem, morph_send_sem, morph_recv_sem,
            share, pull_ref, small_sem, share_send_sem, share_recv_sem, *vmem_refs, load_sem,
        ) = refs
    events, variations = weight.shape
    slots = n_ev * PITCH
    me, my_sys = lax.axis_index("ev"), lax.axis_index("sys")
    barrier = pltpu.get_barrier_semaphore()

    half = n_sys // 2
    first_half = my_sys < half
    partner = n_sys - 1 - my_sys

    shifted, stride = [], 1
    for own, size in zip(digits(me), SIZES):
        shifted.append([lax.rem(own + e, size) * stride for e in range(size)])
        stride = stride * size

    def to(i):
        return {"ev": sum(values[e] for values, e in zip(shifted, digits(PLACES[i])))}

    def greet():
        if later:
            @pl.when(my_sys >= half)
            def _():
                pl.semaphore_signal(barrier, inc=1, device_id={"sys": partner}, device_id_type=MESH)
        else:
            for q in range(n_sys):
                @pl.when(jnp.logical_and(q != my_sys, jnp.logical_or(first_half, q >= half)))
                def _():
                    pl.semaphore_signal(barrier, inc=1, device_id={"sys": q}, device_id_type=MESH)

        for i in range(1, n_ev):
            pl.semaphore_signal(barrier, inc=1, device_id=to(i), device_id_type=MESH)

    def share_copy(sender, target):
        return pltpu.make_async_remote_copy(
            src_ref=share.at[my_sys],
            dst_ref=share.at[my_sys],
            send_sem=share_send_sem.at[target],
            recv_sem=share_recv_sem.at[sender],
            device_id={"sys": target},
            device_id_type=MESH,
        )

    recv[:, K:, :] = jnp.zeros((n_ev, PITCH - K, variations), F32)
    if later:
        greet()
    else:
        pull_copy = pltpu.make_async_copy(pull_hbm, pull_ref, small_sem.at[4])
        pull_copy.start()

        @pl.when(my_sys >= half)
        def _():
            share[0:half] = jnp.zeros((half, 1, events), F32)

        loads = prepare(n_ev, me, hbm_refs, weight, info, vmem_refs, small_sem, load_sem, greet)

    block = info[0:1, :].astype(jnp.int32)
    rank_f = info[1:2, :]
    most = jnp.max(rank_f, axis=1, keepdims=True) + 1.0
    rank = rank_f.astype(jnp.int32)
    if later:
        rank = rank - round_ref[0] * K
    kept = jnp.logical_and(rank >= 0, rank < K)
    slot = jnp.where(kept, block * PITCH + rank, -1)
    rank = jnp.where(kept, rank, -1)
    in_block = iota((n_ev, events), 0) == block
    at_place = onehot(iota((128, events), 0) == rank)
    tags = dot_nt(jnp.where(in_block, info[2:3, :], 0.0).astype(BF16), at_place)
    tags = jnp.where(iota(tags.shape, 1) >= N_LANE, most, tags)

    if not later:
        weigh(loads, weight, info, vmem_refs[0], vmem_refs[1], vmem_refs[5])

        pull_copy.wait()
        var_at = iota((variations, variations // 2), 0)
        mine = iota((variations, variations // 2), 1) == var_at // 2
        pull = jnp.sum(jnp.where(mine, pull_ref[...], 0.0), axis=1, keepdims=True)
        odd = iota((variations, 1), 0) % 2
        coef = jnp.maximum(jnp.where(odd == 0, pull, -pull), 0.0)
        share[my_sys] = jnp.sum(coef * (weight[...].T - info[3:4, :]), axis=0, keepdims=True)

    halves = jnp.concatenate(parts(weight[...], 2), axis=1)
    blocks = n_ev // PACKS
    count = blocks * PITCH

    def fill(p):
        pick = onehot(iota((count, events), 0) + p * count == slot)
        both = dot(pick, halves)
        both = (both[:, :variations] + both[:, variations:]).reshape(blocks, PITCH, variations)
        tag = tags[p * blocks : (p + 1) * blocks, None, :]
        send[pl.ds(p * blocks, blocks)] = jnp.where(iota(both.shape, 1) == K, tag, both)

    def ship(p):
        for i in range(p * blocks, (p + 1) * blocks):
            if i > 0:
                pltpu.make_async_remote_copy(
                    src_ref=send.at[i, pl.ds(0, K + 1)],
                    dst_ref=recv.at[i, pl.ds(0, K + 1)],
                    send_sem=send_sem,
                    recv_sem=recv_sem.at[i * ARRIVALS // n_ev],
                    device_id=to(i),
                    device_id_type=MESH,
                ).start()

    if later:
        pl.semaphore_wait(barrier, n_ev - 1 + jnp.where(first_half, 1, 0))
    else:
        pl.semaphore_wait(barrier, n_ev - 1 + jnp.where(first_half, half - 1, n_sys - 1))
        for q in range(n_sys):
            @pl.when(jnp.logical_and(q != my_sys, jnp.logical_or(my_sys >= half, q < half)))
            def _():
                share_copy(my_sys, q).start()

    fill(0)
    ship(0)
    for p in range(1, FIRST_PACKS):
        fill(p)
        ship(p)
    recv[0, :, :] = send[0, :, :]

    if not later:
        for q in range(n_sys):
            @pl.when(jnp.logical_and(q != my_sys, jnp.logical_or(first_half, q >= half)))
            def _():
                share_copy(q, q).wait_recv()

        info[3:4, :] = info[3:4, :] + sum(share[q] for q in range(1, half)) + share[0]
        info[4:5, :] = sum(share[q] for q in range(half + 1, n_sys)) + share[half]
    pieces = parts(info[3:4, :], 2) + parts(info[4:5, :], 2)
    stacked = [jnp.where(in_block, piece.astype(F32), 0.0).astype(BF16) for piece in pieces]
    row = dot_nt(jnp.concatenate(stacked, axis=0), at_place)
    row = (
        row[:n_ev] + row[n_ev : 2 * n_ev]
        + pltpu.roll(row[2 * n_ev : 3 * n_ev] + row[3 * n_ev :], SECOND_LANE, axis=1)
    )
    terms[...] = row[:, None, :]

    def terms_copy(blocks, peer):
        return pltpu.make_async_remote_copy(
            src_ref=terms.at[blocks], dst_ref=terms_in.at[blocks], send_sem=terms_send_sem,
            recv_sem=terms_recv_sem, device_id=to(peer), device_id_type=MESH,
        )

    for i in range(1, n_ev):
        terms_copy(i, i).start()
    terms_in[0] = terms[0]
    for p in range(FIRST_PACKS, PACKS):
        fill(p)
        ship(p)

    blocks = n_ev // ARRIVALS
    count = blocks * PITCH
    at = iota((1, count), 1)
    place = at % PITCH
    used = place < K
    ours = iota((blocks, count), 0) == at // PITCH
    spread = onehot(jnp.logical_and(iota((128, count), 0) == place, used))

    def flat(rows):
        spaced = dot(rows.astype(BF16), spread).reshape(-1, blocks, count)
        return jnp.sum(jnp.where(ours[None], spaced, 0.0), axis=1)

    def arrived(a):
        first = a * blocks
        some = pl.ds(max(first, 1), first + blocks - max(first, 1))
        pltpu.make_async_remote_copy(
            src_ref=send.at[some, pl.ds(0, K + 1)], dst_ref=recv.at[some, pl.ds(0, K + 1)],
            send_sem=send_sem, recv_sem=recv_sem.at[a], device_id=to(1), device_id_type=MESH,
        ).wait_recv()
        tag = recv[pl.ds(first, blocks), K, :]
        bins = jnp.where(used, flat(tag), -1.0).astype(jnp.int32)
        in_bin = onehot(iota((B, count), 0) == bins)
        picked[:, a * count : (a + 1) * count] = in_bin
        rows = recv[pl.ds(first, blocks)].reshape(count, variations)
        return dot(in_bin, jnp.concatenate(parts(rows, 2), axis=1)), jnp.max(tag[:, N_LANE:], axis=0, keepdims=True)

    total, most = arrived(0)
    for a in range(1, ARRIVALS):
        more_total, more_most = arrived(a)
        total, most = total + more_total, jnp.maximum(most, more_most)
    hist_ref[...] = (total[:, :variations] + total[:, variations:]).T
    if not later:
        most_ref[...] = most

    terms_copy(pl.ds(1, n_ev - 1), 1).wait()
    got = terms_in[:, 0, :]
    pieces = parts(got, 2) + parts(pltpu.roll(got, 128 - SECOND_LANE, axis=1), 2)
    lanes = [
        flat(jnp.concatenate([piece.astype(F32)[a * blocks : (a + 1) * blocks] for piece in pieces], axis=0))
        for a in range(ARRIVALS)
    ]
    lanes = jnp.concatenate([jnp.concatenate(lanes, axis=1), jnp.zeros((4, slots), F32)], axis=0)
    morphed = dot_nt(lanes.astype(BF16), picked[...])
    morph_copy = pltpu.make_async_remote_copy(
        src_ref=morph, dst_ref=morph, send_sem=morph_send_sem, recv_sem=morph_recv_sem,
        device_id={"sys": partner}, device_id_type=MESH,
    )

    @pl.when(first_half)
    def _():
        morph[...] = morphed[0:1] + morphed[1:2]
        morph_copy.start()

    @pl.when(my_sys >= half)
    def _():
        morph_copy.wait_recv()

    expected_ref[...] = morph[...] + (morphed[2:3] + morphed[3:4])

    sent = pl.ds(1, n_ev - 1)
    pltpu.make_async_remote_copy(
        src_ref=send.at[sent, pl.ds(0, K + 1)], dst_ref=recv.at[sent, pl.ds(0, K + 1)],
        send_sem=send_sem, recv_sem=recv_sem.at[0], device_id=to(1), device_id_type=MESH,
    ).wait_send()
    @pl.when(first_half)
    def _():
        morph_copy.wait_send()

    if not later:
        for q in range(n_sys):
            @pl.when(jnp.logical_and(q != my_sys, jnp.logical_or(my_sys >= half, q < half)))
            def _():
                share_copy(my_sys, q).wait_send()


def in_hbm(x):
    return pltpu.with_memory_space_constraint(x, pltpu.HBM)


def store(hist_ref, expected_ref, templates_hbm, expected_hbm, sem):
    copies = (
        pltpu.make_async_copy(hist_ref, templates_hbm.at[0], sem.at[0]),
        pltpu.make_async_copy(expected_ref, expected_hbm, sem.at[1]),
    )
    for copy in copies:
        copy.start()
    for copy in copies:
        copy.wait()


def finish(templates, expected):
    vmem = pl.BlockSpec(memory_space=pltpu.VMEM)
    hbm = pl.BlockSpec(memory_space=pltpu.HBM)
    return pl.pallas_call(
        store,
        out_shape=(
            jax.ShapeDtypeStruct((1,) + templates.shape, F32),
            jax.ShapeDtypeStruct(expected.shape, F32),
        ),
        in_specs=[vmem] * 2,
        out_specs=(hbm, hbm),
        scratch_shapes=[pltpu.SemaphoreType.DMA((2,))],
        name="store",
    )(templates, expected)


def local(n_ev, n_sys, observables, selection, base_weight, category, bin_number, response, nuisance_pulls):
    events, features = observables.shape
    variations = response.shape[1]
    vmem = pl.BlockSpec(memory_space=pltpu.VMEM)
    hbm = pl.BlockSpec(memory_space=pltpu.HBM)
    slots = n_ev * PITCH
    results = (
        jax.ShapeDtypeStruct((variations, B), F32),
        jax.ShapeDtypeStruct((1, B), F32),
    )
    scratch = [
        pltpu.VMEM((n_ev, PITCH, variations), F32),
        pltpu.VMEM((n_ev, PITCH, variations), F32),
        pltpu.VMEM((n_ev, 1, 128), F32),
        pltpu.VMEM((n_ev, 1, 128), F32),
        pltpu.VMEM((B, slots), BF16),
        pltpu.VMEM((1, B), F32),
        pltpu.SemaphoreType.DMA,
        pltpu.SemaphoreType.DMA((ARRIVALS,)),
        pltpu.SemaphoreType.DMA,
        pltpu.SemaphoreType.DMA,
        pltpu.SemaphoreType.DMA,
        pltpu.SemaphoreType.DMA,
    ]
    templates, expected, most, weight, info = pl.pallas_call(
        functools.partial(exchange, n_ev, n_sys, False),
        out_shape=results + (
            jax.ShapeDtypeStruct((1, 128 - N_LANE), F32),
            jax.ShapeDtypeStruct((events, variations), F32),
            jax.ShapeDtypeStruct((8, events), F32),
        ),
        in_specs=[hbm] * 7,
        out_specs=(vmem,) * 5,
        scratch_shapes=scratch + [
            pltpu.VMEM((n_sys, 1, events), F32),
            pltpu.VMEM((1, variations // 2), F32),
            pltpu.SemaphoreType.DMA((5,)),
            pltpu.SemaphoreType.DMA((n_sys,)),
            pltpu.SemaphoreType.DMA((n_sys,)),
            pltpu.VMEM((events, features), BF16),
            pltpu.VMEM((events, features), jnp.int32),
            pltpu.VMEM((1, events), F32),
            pltpu.VMEM((1, events), jnp.int32),
            pltpu.VMEM((1, events), jnp.int32),
            pltpu.VMEM((features, variations), BF16),
            pltpu.SemaphoreType.DMA((2, STEPS)),
        ],
        compiler_params=pltpu.CompilerParams(
            collective_id=0, has_side_effects=True, vmem_limit_bytes=VMEM_BYTES
        ),
        name="first_round",
    )(
        in_hbm(observables),
        in_hbm(selection),
        in_hbm(base_weight.reshape(1, events)),
        in_hbm(category.reshape(1, events)),
        in_hbm(bin_number.reshape(1, events)),
        in_hbm(response),
        in_hbm(nuisance_pulls.reshape(1, -1)),
    )
    largest = most[0, 0].astype(jnp.int32)

    def more(carry):
        return carry[0] * K < largest

    def next_round(carry):
        index, templates, expected = carry
        extra, extra_expected = pl.pallas_call(
            functools.partial(exchange, n_ev, n_sys, True),
            out_shape=results,
            in_specs=[pl.BlockSpec(memory_space=pltpu.SMEM), vmem, vmem],
            out_specs=(vmem, vmem),
            scratch_shapes=scratch,
            compiler_params=pltpu.CompilerParams(
                collective_id=1, has_side_effects=True, vmem_limit_bytes=VMEM_BYTES
            ),
            name="later_round",
        )(index.reshape(1), weight, info)
        return index + 1, templates + extra, expected + extra_expected

    _, templates, expected = lax.while_loop(more, next_round, (jnp.int32(1), templates, expected))
    return finish(templates, expected)


def solution(mesh):
    placed = (P("ev", None), P("ev", None), P("ev"), P("ev"), P("ev"), P(None, "sys"), P("sys"))
    return jax.shard_map(
        functools.partial(local, mesh.shape["ev"], mesh.shape["sys"]),
        mesh=mesh,
        in_specs=placed,
        out_specs=(P("ev", "sys", None), P("ev", None)),
        check_vma=False,
    )
```
